128 devices in a mesh: ctx: 128 (over y, z, x, core).
Axes of the slice: x: 4, y: 4, z: 4, core: 2. Of those that a mesh axis runs over, the one named last changes fastest.
Arguments:
- queries: bfloat16 [131072, 2048], P('ctx'), may hold values from -6 to 6
- keys: bfloat16 [131072, 2048], P('ctx'), may hold values from -6 to 6
- values: bfloat16 [131072, 2048], P('ctx'), may hold values from -6 to 6
- level_gate: bfloat16 [131072, 128], P('ctx'), may hold values from 0.19921875 to 2
- norm_gain: float32 [2048], replicated, may hold values from 0.5 to 1.5
- out_weight: bfloat16 [2048, 2048], P('ctx'), may hold values from -0.125 to 0.125
Outputs:
- layer_out: bfloat16 [131072, 2048], P('ctx')
The draws below stay inside these ranges and needn't reach their ends.
All inputs are finite; a program needn't handle non-finite values.
Results may differ from the reference program's by a relative error of at most 0.0057.
Values may be sent and summed in bfloat16 or wider, within the bound.
No kernel may reach another device: no remote copies, remote signals or barrier semaphores. Data moves between devices by JAX's collectives and lax.ppermute only.
A program may use at most 192 MiB of HBM per device.

```python
import math
import jax
import jax.numpy as jnp
from jax import lax

HEADS = 16
HEAD = 128
D = 2048
TOK_DEV = 1024
GATES = 8
TOKENS = 131072
N_CTX = 128


def block_levels(rng, dims, split, smallest, top_value):
    def one(dim, blocks):
        draws = jax.random.uniform(jax.random.fold_in(jax.random.fold_in(rng, 6), dim), (blocks,), jnp.float32, smallest / len(split), top_value / len(split))
        return jnp.repeat(jnp.exp(draws), dims[dim] // blocks).reshape((-1,) + (1,) * (len(dims) - dim - 1))

    loudness = one(*split[0])
    for cut in split[1:]:
        loudness = loudness * one(*cut)
    return loudness


def normal_values(key, dims, width, most, split=(), held_as=jnp.bfloat16):
    result = width * jax.random.normal(key, dims, jnp.float32)
    if split:
        result = result * block_levels(key, dims, split, -0.22, 0.18)
    return jnp.clip(result, -most, most).astype(held_as)


def setup_inputs(seed: int = 0) -> dict:
    seeds = jax.random.split(jax.random.key(seed), 7)
    queries = normal_values(seeds[0], (TOKENS, D), 1.0, 6.0, ((0, 128),))
    keys = normal_values(seeds[1], (TOKENS, D), 1.0, 6.0, ((0, 128),))
    values = normal_values(seeds[2], (TOKENS, D), 1.0, 6.0, ((0, 128),))
    level_gate = jnp.clip(jnp.exp(math.log(2.0) - 2.306499 * jax.random.uniform(seeds[3], (TOKENS, GATES * HEADS), jnp.float32) ** block_levels(seeds[3], (TOKENS, GATES * HEADS), ((0, 128),), -0.2, 0.2)), 0.19921875, 2.0).astype(jnp.bfloat16)
    norm_gain = jnp.clip(1.0 + 0.1 * jax.random.normal(seeds[4], (D,), jnp.float32), 0.5, 1.5)
    out_weight = normal_values(seeds[5], (D, D), D ** -0.5, 0.125, ((0, 128),))
    return dict(queries=queries, keys=keys, values=values, level_gate=level_gate, norm_gain=norm_gain, out_weight=out_weight)


EPSILON = 1e-06
HIGH = lax.Precision.HIGHEST

def within_shard(query_heads, key_heads, value_heads, level_weights):
    scores = jnp.einsum('thd,shd->hts', query_heads.astype(jnp.float32), key_heads.astype(jnp.float32), precision=HIGH)
    positions = jnp.arange(query_heads.shape[0], dtype=jnp.int32)
    causal = positions[:, None] >= positions[None, :]
    weighted = jnp.where(causal[None], scores, jnp.float32(0.0)).astype(jnp.bfloat16)
    mixed = jnp.einsum('hts,shd->thd', weighted.astype(jnp.float32), value_heads.astype(jnp.float32), precision=HIGH)
    return mixed * level_weights[:, 0, :, None]

def finish(summed, norm_gain):
    squares = lax.optimization_barrier(jnp.mean(summed * summed, axis=-1, keepdims=True))
    normed = summed * lax.rsqrt(squares + EPSILON) * norm_gain.reshape(HEADS, HEAD)
    return normed.reshape(summed.shape[0], HEADS * HEAD).astype(jnp.bfloat16)

def reference(queries, keys, values, level_gate, norm_gain, out_weight):
    shards = N_CTX
    levels = shards.bit_length() - 1
    query_all = queries.reshape(shards, TOK_DEV, HEADS, HEAD)
    key_all = keys.reshape(shards, TOK_DEV, HEADS, HEAD)
    value_all = values.reshape(shards, TOK_DEV, HEADS, HEAD)
    weight_all = level_gate.reshape(shards, TOK_DEV, GATES, HEADS).astype(jnp.float32)

    def shard_state(pair):
        return jnp.einsum('shd,she->hde', pair[0].astype(jnp.float32), pair[1].astype(jnp.float32), precision=HIGH)
    states = lax.map(shard_state, (key_all, value_all))
    tables = [states.reshape(shards >> level_index, 1 << level_index, HEADS, HEAD, HEAD).sum(1) for level_index in range(levels)]

    def one_shard(position):
        query_heads = query_all[position]
        level_weights = weight_all[position]
        summed = within_shard(query_heads, key_all[position], value_all[position], level_weights)
        for level_index in range(levels):
            upper_half = position >> level_index & 1 == 1
            block = jnp.maximum((position >> level_index) - 1, 0)
            bucket = jnp.where(upper_half, tables[level_index][block], jnp.float32(0.0)).astype(jnp.bfloat16)
            product = jnp.einsum('thd,hde->the', query_heads.astype(jnp.float32), bucket.astype(jnp.float32), precision=HIGH)
            summed = summed + level_weights[:, level_index + 1, :, None] * product
        return finish(summed, norm_gain)
    mixed = lax.map(one_shard, jnp.arange(shards, dtype=jnp.int32))
    mixed = mixed.reshape(shards * TOK_DEV, HEADS * HEAD)
    return jnp.dot(mixed, out_weight, preferred_element_type=jnp.float32).astype(jnp.bfloat16)
```

```python
import functools

import jax
import jax.numpy as jnp
from jax import lax
from jax.experimental import pallas as pl
from jax.experimental.pallas import tpu as pltpu
from jax.sharding import PartitionSpec as P

HEADS = 16
HEAD = 128
GATES = 8
HALF = HEADS // 2
ROWS = 1024
CHUNK = 256
CHUNKS = ROWS // CHUNK
EPSILON = 1e-06
VMEM_MIB = 60
F32 = jnp.float32
BF16 = jnp.bfloat16


def params(mib, **more):
    return pltpu.CompilerParams(vmem_limit_bytes=mib << 20, **more)


def cost(flops, moved):
    return pl.CostEstimate(flops=int(flops), bytes_accessed=int(moved), transcendentals=0)


def dot(a, b, contract=((1,), (0,))):
    return lax.dot_general(a, b, (contract, ((), ())), preferred_element_type=F32)


def state_body(k_ref, v_ref, total_ref, sent_ref, prefix_ref):
    for pair in range(2):
        cols = slice(pair * HEAD, (pair + 1) * HEAD)
        total = None
        for c in range(CHUNKS):
            rows = slice(c * CHUNK, (c + 1) * CHUNK)
            part = dot(k_ref[rows, cols], v_ref[rows, cols], ((0,), (0,)))
            total = part if total is None else total + part
            if c + 1 < CHUNKS:
                prefix_ref[pair, c] = total.astype(BF16)
        total_ref[pair] = total
        sent_ref[pair] = total.astype(BF16)


def states(keys, values):
    block = pl.BlockSpec((ROWS, 2 * HEAD), lambda i: (0, i))
    square = pl.BlockSpec((2, HEAD, HEAD), lambda i: (i, 0, 0))
    return pl.pallas_call(
        state_body,
        grid=(HEADS // 2,),
        in_specs=[block, block],
        out_specs=[square, square, pl.BlockSpec((2, CHUNKS - 1, HEAD, HEAD), lambda i: (i, 0, 0, 0))],
        out_shape=[
            jax.ShapeDtypeStruct((HEADS, HEAD, HEAD), F32),
            jax.ShapeDtypeStruct((HEADS, HEAD, HEAD), BF16),
            jax.ShapeDtypeStruct((HEADS, CHUNKS - 1, HEAD, HEAD), BF16),
        ],
        compiler_params=params(VMEM_MIB),
        cost_estimate=cost(2 * ROWS * HEAD * HEAD * HEADS, 10 << 20),
        name="states",
    )(keys, values)


def local_body(side, s_ref, q_ref, k_ref, v_ref, prefix_ref, gate_ref, out_ref):
    core = s_ref[0] if side == 0 else 1 - s_ref[0]
    first = core * HALF + 2 * pl.program_id(0)
    causal = lax.broadcasted_iota(jnp.int32, (CHUNK, CHUNK), 0) >= lax.broadcasted_iota(
        jnp.int32, (CHUNK, CHUNK), 1
    )
    for pair in range(2):
        cols = slice(pair * HEAD, (pair + 1) * HEAD)
        shift = lax.rem(HEAD - (first + pair), HEAD)
        for c in range(CHUNKS):
            rows = slice(c * CHUNK, (c + 1) * CHUNK)
            q = q_ref[rows, cols]
            scores = dot(q, k_ref[rows, cols], ((1,), (1,)))
            scores = jnp.where(causal, scores, 0.0).astype(BF16)
            mixed = dot(scores, v_ref[rows, cols])
            if c:
                mixed = mixed + dot(q, prefix_ref[pair, c - 1])
            weight = pltpu.roll(gate_ref[rows, :].astype(F32), shift, 1)[:, 0:1]
            out_ref[rows, cols] = mixed * weight


def local(side, scalars, queries, keys, values, prefix, level_gate):
    quarter = HALF // 2
    where = lambda i, s: (s[0] if side == 0 else 1 - s[0]) * quarter + i
    block = pl.BlockSpec((ROWS, 2 * HEAD), lambda i, s: (0, where(i, s)))
    return pl.pallas_call(
        functools.partial(local_body, side),
        grid_spec=pltpu.PrefetchScalarGridSpec(
            num_scalar_prefetch=1,
            grid=(quarter,),
            in_specs=[
                block,
                block,
                block,
                pl.BlockSpec((2, CHUNKS - 1, HEAD, HEAD), lambda i, s: (where(i, s), 0, 0, 0)),
                pl.BlockSpec((ROWS, GATES * HEADS), lambda i, s: (0, 0)),
            ],
            out_specs=pl.BlockSpec((ROWS, 2 * HEAD), lambda i, s: (0, i)),
        ),
        out_shape=jax.ShapeDtypeStruct((ROWS, HALF * HEAD), F32),
        compiler_params=params(VMEM_MIB),
        cost_estimate=cost(4e9, 11 << 20),
        name=f"local{side}",
    )(scalars, queries, keys, values, prefix, level_gate)


def add_levels(scalars, head, q, gate, attended, levels, buckets):
    shift = lax.rem(HEAD - head, HEAD)
    rolled = pltpu.roll(gate, shift, 1)
    at = 0
    while at < len(levels):
        group = levels[at : at + 2]
        square = jnp.concatenate(buckets[at : at + 2], axis=1)
        product = dot(q, square)
        for n, level in enumerate(group):
            flag = scalars[1 + level].astype(F32)
            column = (level + 1) * HEADS
            weight = rolled[:, column : column + 1] * flag
            attended = attended + product[:, n * HEAD : (n + 1) * HEAD] * weight
        at += 2
    return attended


def head_maps():
    mine = lambda i, s: s[0] * HALF + i
    yours = lambda i, s: (1 - s[0]) * HALF + i
    return mine, yours


def final_body(levels, s_ref, q0, q1, a0, a1, gate_ref, gain_ref, *refs):
    buckets = refs[: 2 * len(levels)]
    weight_ref, out_ref, normed_ref = refs[2 * len(levels) :]
    i = pl.program_id(0)
    core = s_ref[0]

    @pl.when(i < HALF)
    def _():
        for side, (q, a) in enumerate(((q0, a0), (q1, a1))):
            head = (core if side == 0 else 1 - core) * HALF + i
            squares = [buckets[2 * n + side][0] for n in range(len(levels))]
            gain = gain_ref[pl.ds(head, 1), :]
            cols = pl.ds(pl.multiple_of(head * HEAD, HEAD), HEAD)
            for c in range(CHUNKS):
                rows = slice(c * CHUNK, (c + 1) * CHUNK)
                x = add_levels(
                    s_ref, head, q[rows, :], gate_ref[rows, :].astype(F32), a[rows, :], levels, squares
                )
                squares_mean = jnp.mean(x * x, axis=1, keepdims=True)
                normed_ref[rows, cols] = (x * lax.rsqrt(squares_mean + EPSILON) * gain).astype(BF16)

    @pl.when(i >= HALF)
    def _():
        out_ref[...] = dot(normed_ref[...], weight_ref[...]).astype(BF16)


def final(scalars, queries, attended, level_gate, gain, levels, buckets, weight):
    mine, yours = head_maps()
    clip = lambda i: jnp.minimum(i, HALF - 1)
    tile = HEADS * HEAD // HALF
    col0 = lambda i, s: (0, mine(clip(i), s))
    col1 = lambda i, s: (0, yours(clip(i), s))
    own = pl.BlockSpec((1, HEAD, HEAD), lambda i, s: (clip(i), 0, 0))
    specs = []
    for level in levels:
        if level == 0:
            specs += [
                pl.BlockSpec((1, HEAD, HEAD), lambda i, s: (mine(clip(i), s), 0, 0)),
                pl.BlockSpec((1, HEAD, HEAD), lambda i, s: (yours(clip(i), s), 0, 0)),
            ]
        else:
            specs += [own, own]
    late = lambda i, s: (0, jnp.maximum(i - HALF, 0))
    return pl.pallas_call(
        functools.partial(final_body, levels),
        grid_spec=pltpu.PrefetchScalarGridSpec(
            num_scalar_prefetch=1,
            grid=(2 * HALF,),
            in_specs=[
                pl.BlockSpec((ROWS, HEAD), col0),
                pl.BlockSpec((ROWS, HEAD), col1),
                pl.BlockSpec((ROWS, HEAD), lambda i, s: (0, clip(i))),
                pl.BlockSpec((ROWS, HEAD), lambda i, s: (0, clip(i))),
                pl.BlockSpec((ROWS, GATES * HEADS), lambda i, s: (0, 0)),
                pl.BlockSpec((HEADS, HEAD), lambda i, s: (0, 0)),
                *specs,
                pl.BlockSpec((HEADS * HEAD, tile), late),
            ],
            out_specs=pl.BlockSpec((ROWS, tile), late),
            scratch_shapes=[pltpu.VMEM((ROWS, HEADS * HEAD), BF16)],
        ),
        out_shape=jax.ShapeDtypeStruct((ROWS, HEADS * HEAD), BF16),
        compiler_params=params(VMEM_MIB),
        cost_estimate=cost(13e9, 30 << 20),
        name="final",
    )(scalars, queries, queries, *attended, level_gate, gain, *buckets, weight)


def from_partner(value, axis, bit):
    mask = 2**bit
    pairs = [(source, source ^ mask) for source in range(lax.axis_size(axis))]
    return lax.ppermute(value, axis, pairs)


def shards(queries, keys, values, level_gate, norm_gain, out_weight):
    position = lax.axis_index("ctx")
    levels = lax.axis_size("ctx").bit_length() - 1
    core = position & 1
    scalars = jnp.stack([core] + [position >> level & 1 for level in range(levels)]).astype(jnp.int32)
    whole_weight = lax.all_gather(out_weight, "ctx", axis=0, tiled=True)
    total, sent, prefix = states(keys, values)
    first = from_partner(sent, "ctx", 0)
    attended = [None, None]
    buckets = [first, first]
    running = lax.dynamic_slice_in_dim(total, core * HALF, HALF) + lax.dynamic_slice_in_dim(
        first, core * HALF, HALF
    ).astype(F32)
    for level in range(1, levels):
        outgoing = running.astype(BF16)
        if level == 1:
            outgoing, q_a = lax.optimization_barrier((outgoing, queries))
            attended[0] = local(0, scalars, q_a, keys, values, prefix, level_gate)
        if level == 3:
            outgoing, q_b, attended[0] = lax.optimization_barrier((outgoing, queries, attended[0]))
            attended[1] = local(1, scalars, q_b, keys, values, prefix, level_gate)
        if level == 5:
            outgoing, attended[1] = lax.optimization_barrier((outgoing, attended[1]))
        received = from_partner(outgoing, "ctx", level)
        other = from_partner(received, "ctx", 0)
        buckets += [received, other]
        if level + 1 < levels:
            running = running + received.astype(F32)
    gain = norm_gain.reshape(HEADS, HEAD)
    return final(
        scalars, queries, attended, level_gate, gain, list(range(levels)), buckets, whole_weight
    )


def solution(mesh):
    placed = (P("ctx", None), P("ctx", None), P("ctx", None), P("ctx", None), P(), P("ctx", None))
    return jax.shard_map(
        shards, mesh=mesh, in_specs=placed, out_specs=P("ctx", None), check_vma=False
    )
```

```python
import functools

import jax
import jax.numpy as jnp
from jax import lax
from jax.experimental import pallas as pl
from jax.experimental.pallas import tpu as pltpu
from jax.sharding import PartitionSpec as P

HEADS = 16
HEAD = 128
GATES = 8
HALF = HEADS // 2
QUARTER = HEADS // 4
ROWS = 1024
CHUNK = 256
CHUNKS = ROWS // CHUNK
EPSILON = 1e-06
VMEM_MIB = 60
F32 = jnp.float32
BF16 = jnp.bfloat16
NN = ((1,), (0,))
NT = ((1,), (1,))


def params():
    return pltpu.CompilerParams(vmem_limit_bytes=VMEM_MIB << 20)


def cost(flops, moved):
    return pl.CostEstimate(flops=int(flops), bytes_accessed=int(moved), transcendentals=0)


def dot(a, b, contract=NN):
    return lax.dot_general(a, b, (contract, ((), ())), preferred_element_type=F32)


def state_body(k_ref, v_ref, total_ref, sent_ref, prefix_ref, vt_ref):
    for pair in range(2):
        cols = slice(pair * HEAD, (pair + 1) * HEAD)
        vt = jnp.transpose(v_ref[:, cols])
        vt_ref[cols, :] = vt
        total = None
        for c in range(CHUNKS):
            rows = slice(c * CHUNK, (c + 1) * CHUNK)
            part = dot(vt[:, rows], k_ref[rows, cols])
            total = part if total is None else total + part
            if c + 1 < CHUNKS:
                prefix_ref[pair, c] = total.astype(BF16)
        total_ref[pair] = total
        sent_ref[pair] = total.astype(BF16)


def states(keys, values):
    block = pl.BlockSpec((ROWS, 2 * HEAD), lambda i: (0, i))
    square = pl.BlockSpec((2, HEAD, HEAD), lambda i: (i, 0, 0))
    return pl.pallas_call(
        state_body,
        grid=(HEADS // 2,),
        in_specs=[block, block],
        out_specs=[
            square,
            square,
            pl.BlockSpec((2, CHUNKS - 1, HEAD, HEAD), lambda i: (i, 0, 0, 0)),
            pl.BlockSpec((2 * HEAD, ROWS), lambda i: (i, 0)),
        ],
        out_shape=[
            jax.ShapeDtypeStruct((HEADS, HEAD, HEAD), F32),
            jax.ShapeDtypeStruct((HEADS, HEAD, HEAD), BF16),
            jax.ShapeDtypeStruct((HEADS, CHUNKS - 1, HEAD, HEAD), BF16),
            jax.ShapeDtypeStruct((HEADS * HEAD, ROWS), BF16),
        ],
        compiler_params=params(),
        cost_estimate=cost(1e9, 14 << 20),
        name="states",
    )(keys, values)


def side_of(side, core):
    return core if side == 0 else 1 - core


def local_body(side, s_ref, q_ref, k_ref, vt_ref, prefix_ref, first_ref, gate_ref, out_ref):
    head0 = side_of(side, s_ref[0]) * HALF + 2 * pl.program_id(0)
    causal = lax.broadcasted_iota(jnp.int32, (CHUNK, CHUNK), 0) <= lax.broadcasted_iota(
        jnp.int32, (CHUNK, CHUNK), 1
    )
    for pair in range(2):
        cols = slice(pair * HEAD, (pair + 1) * HEAD)
        w0 = gate_ref[pl.ds(head0 + pair, 1), :]
        w1 = gate_ref[pl.ds(HEADS + head0 + pair, 1), :]
        for c in range(CHUNKS):
            rows = slice(c * CHUNK, (c + 1) * CHUNK)
            q = q_ref[rows, cols]
            scores = dot(k_ref[rows, cols], q, NT)
            scores = jnp.where(causal, scores, 0.0).astype(BF16)
            mixed = dot(vt_ref[cols, rows], scores)
            if c:
                both = jnp.concatenate([prefix_ref[pair, c - 1], first_ref[pair]], axis=0)
                both = dot(both, q, NT)
                mixed = mixed + both[:HEAD]
                level = both[HEAD:]
            else:
                level = dot(first_ref[pair], q, NT)
            out_ref[cols, rows] = mixed * w0[:, rows] + level * w1[:, rows]


def local(side, scalars, queries, keys, vt, prefix, first, gate):
    where = lambda i, s: side_of(side, s[0]) * QUARTER + i
    block = pl.BlockSpec((ROWS, 2 * HEAD), lambda i, s: (0, where(i, s)))
    return pl.pallas_call(
        functools.partial(local_body, side),
        grid_spec=pltpu.PrefetchScalarGridSpec(
            num_scalar_prefetch=1,
            grid=(QUARTER,),
            in_specs=[
                block,
                block,
                pl.BlockSpec((2 * HEAD, ROWS), lambda i, s: (where(i, s), 0)),
                pl.BlockSpec((2, CHUNKS - 1, HEAD, HEAD), lambda i, s: (where(i, s), 0, 0, 0)),
                pl.BlockSpec((2, HEAD, HEAD), lambda i, s: (where(i, s), 0, 0)),
                pl.BlockSpec((GATES * HEADS, ROWS), lambda i, s: (0, 0)),
            ],
            out_specs=pl.BlockSpec((2 * HEAD, ROWS), lambda i, s: (i, 0)),
        ),
        out_shape=jax.ShapeDtypeStruct((HALF * HEAD, ROWS), F32),
        compiler_params=params(),
        cost_estimate=cost(4e9, 11 << 20),
        name=f"local{side}",
    )(scalars, queries, keys, vt, prefix, first, gate)


def with_levels(head, levels, squares, q, gate_ref, rows, attended):
    products = dot(squares, q, NT)
    for n, level in enumerate(levels):
        weight = gate_ref[pl.ds((level + 1) * HEADS + head, 1), rows]
        attended = attended + products[n * HEAD : (n + 1) * HEAD] * weight
    return attended


def partial_body(side, levels, s_ref, q_ref, a_ref, gate_ref, *refs):
    *buckets, out_ref = refs
    head0 = side_of(side, s_ref[0]) * HALF + 2 * pl.program_id(0)
    for pair in range(2):
        cols = slice(pair * HEAD, (pair + 1) * HEAD)
        squares = jnp.concatenate([b[pair] for b in buckets], axis=0)
        for c in range(CHUNKS):
            rows = slice(c * CHUNK, (c + 1) * CHUNK)
            out_ref[cols, rows] = with_levels(
                head0 + pair, levels, squares, q_ref[rows, cols], gate_ref, rows, a_ref[cols, rows]
            )


def side_specs(side, levels):
    where = lambda i, s: side_of(side, s[0]) * QUARTER + i
    return [
        pl.BlockSpec((ROWS, 2 * HEAD), lambda i, s: (0, where(i, s))),
        pl.BlockSpec((2 * HEAD, ROWS), lambda i, s: (i, 0)),
        pl.BlockSpec((GATES * HEADS, ROWS), lambda i, s: (0, 0)),
        *[pl.BlockSpec((2, HEAD, HEAD), lambda i, s: (i, 0, 0)) for _ in levels],
    ]


def partial_levels(side, levels, scalars, queries, attended, gate, buckets):
    return pl.pallas_call(
        functools.partial(partial_body, side, levels),
        grid_spec=pltpu.PrefetchScalarGridSpec(
            num_scalar_prefetch=1,
            grid=(QUARTER,),
            in_specs=side_specs(side, levels),
            out_specs=pl.BlockSpec((2 * HEAD, ROWS), lambda i, s: (i, 0)),
        ),
        out_shape=jax.ShapeDtypeStruct((HALF * HEAD, ROWS), F32),
        compiler_params=params(),
        cost_estimate=cost(2e9, 10 << 20),
        name=f"levels{side}",
    )(scalars, queries, attended, gate, *buckets)


def norm_body(levels, s_ref, *refs):
    count = len(levels)
    gain_ref, out0_ref, out1_ref = refs[-3:]
    step = pl.program_id(0)
    core = s_ref[0]
    for side, out_ref in ((0, out0_ref), (1, out1_ref)):
        q_ref, a_ref, gate_ref, *buckets = refs[side * (3 + count) : (side + 1) * (3 + count)]
        for pair in range(2):
            head = side_of(side, core) * HALF + 2 * step + pair
            cols = slice(pair * HEAD, (pair + 1) * HEAD)
            squares = jnp.concatenate([b[pair] for b in buckets], axis=0)
            gain = gain_ref[pl.ds(head, 1), :]
            for c in range(CHUNKS):
                rows = slice(c * CHUNK, (c + 1) * CHUNK)
                x = with_levels(head, levels, squares, q_ref[rows, cols], gate_ref, rows, a_ref[cols, rows])
                mean = jnp.mean(x * x, axis=0, keepdims=True)
                x = jnp.transpose(x * lax.rsqrt(mean + EPSILON))
                out_ref[rows, cols] = (x * gain).astype(BF16)


def normed(levels, scalars, queries, attended, gate, buckets, gain):
    half = jax.ShapeDtypeStruct((ROWS, HALF * HEAD), BF16)
    out = pl.BlockSpec((ROWS, 2 * HEAD), lambda i, s: (0, i))
    operands = []
    for side in range(2):
        operands += [queries, attended[side], gate, *buckets[side]]
    return pl.pallas_call(
        functools.partial(norm_body, levels),
        grid_spec=pltpu.PrefetchScalarGridSpec(
            num_scalar_prefetch=1,
            grid=(QUARTER,),
            in_specs=[
                *side_specs(0, levels),
                *side_specs(1, levels),
                pl.BlockSpec((HEADS, HEAD), lambda i, s: (0, 0)),
            ],
            out_specs=[out, out],
        ),
        out_shape=[half, half],
        compiler_params=params(),
        cost_estimate=cost(4e9, 18 << 20),
        name="normed",
    )(scalars, *operands, gain)


def project_body(s_ref, n0_ref, n1_ref, w0_ref, w1_ref, out_ref):
    out_ref[...] = (dot(n0_ref[...], w0_ref[...]) + dot(n1_ref[...], w1_ref[...])).astype(BF16)


def project(scalars, halves, weight):
    tile = 256
    depth = HALF * HEAD
    whole = pl.BlockSpec((ROWS, depth), lambda i, s: (0, 0))
    return pl.pallas_call(
        project_body,
        grid_spec=pltpu.PrefetchScalarGridSpec(
            num_scalar_prefetch=1,
            grid=(HEADS * HEAD // tile,),
            in_specs=[
                whole,
                whole,
                pl.BlockSpec((depth, tile), lambda i, s: (s[0], i)),
                pl.BlockSpec((depth, tile), lambda i, s: (1 - s[0], i)),
            ],
            out_specs=pl.BlockSpec((ROWS, tile), lambda i, s: (0, i)),
        ),
        out_shape=jax.ShapeDtypeStruct((ROWS, HEADS * HEAD), BF16),
        compiler_params=params(),
        cost_estimate=cost(8e9, 16 << 20),
        name="project",
    )(scalars, *halves, weight, weight)


def from_partner(value, axis, bit):
    mask = 2**bit
    pairs = [(source, source ^ mask) for source in range(lax.axis_size(axis))]
    return lax.ppermute(value, axis, pairs)


def shards(queries, keys, values, level_gate, norm_gain, out_weight):
    position = lax.axis_index("ctx")
    levels = lax.axis_size("ctx").bit_length() - 1
    core = position & 1
    scalars = core.astype(jnp.int32).reshape(1)
    whole_weight = lax.all_gather(out_weight, "ctx", axis=0, tiled=True)
    bits = position >> jnp.arange(levels, dtype=jnp.int32) & 1
    present = jnp.concatenate([jnp.ones((1,), F32), bits.astype(F32)])
    gate = level_gate.T.astype(F32) * jnp.repeat(present, HEADS)[:, None]
    total, sent, prefix, vt = states(keys, values)
    first = from_partner(sent, "ctx", 0)
    attended = [None, None]
    mine, yours = {}, {}
    running = lax.dynamic_slice_in_dim(total, core * HALF, HALF) + lax.dynamic_slice_in_dim(
        first, core * HALF, HALF
    ).astype(F32)
    early = [1, 2, 3]
    late = [4, 5, 6]
    for level in range(1, levels):
        outgoing = running.astype(BF16)
        if level == 1:
            outgoing, q = lax.optimization_barrier((outgoing, queries))
            attended[0] = local(0, scalars, q, keys, vt, prefix, first, gate)
        if level == 2:
            outgoing, q = lax.optimization_barrier((outgoing, queries))
            attended[1] = local(1, scalars, q, keys, vt, prefix, first, gate)
        if level == 3:
            outgoing, attended[0] = lax.optimization_barrier((outgoing, attended[0]))
        if level == 4:
            outgoing, attended[1] = lax.optimization_barrier((outgoing, attended[1]))
        if level == 5:
            outgoing, q = lax.optimization_barrier((outgoing, queries))
            attended[0] = partial_levels(0, early, scalars, q, attended[0], gate, [mine[l] for l in early])
        if level == 6:
            outgoing, q, attended[0] = lax.optimization_barrier((outgoing, queries, attended[0]))
            attended[1] = partial_levels(1, early, scalars, q, attended[1], gate, [yours[l] for l in early])
        received = from_partner(outgoing, "ctx", level)
        mine[level] = received
        yours[level] = from_partner(received, "ctx", 0)
        if level + 1 < levels:
            running = running + received.astype(F32)
    gain = norm_gain.reshape(HEADS, HEAD)
    buckets = [[mine[l] for l in late], [yours[l] for l in late]]
    halves = normed(late, scalars, queries, attended, gate, buckets, gain)
    return project(scalars, halves, whole_weight)


def solution(mesh):
    placed = (P("ctx", None), P("ctx", None), P("ctx", None), P("ctx", None), P(), P("ctx", None))
    return jax.shard_map(
        shards, mesh=mesh, in_specs=placed, out_specs=P("ctx", None), check_vma=False
    )
```

```python
import functools

import jax
import jax.numpy as jnp
from jax import lax
from jax.experimental import pallas as pl
from jax.experimental.pallas import tpu as pltpu
from jax.sharding import PartitionSpec as P

HEADS = 16
HEAD = 128
GATES = 8
HALF = HEADS // 2
QUARTER = HEADS // 4
ROWS = 1024
CHUNK = 256
CHUNKS = ROWS // CHUNK
EPSILON = 1e-06
VMEM_MIB = 60
F32 = jnp.float32
BF16 = jnp.bfloat16
NN = ((1,), (0,))
NT = ((1,), (1,))


def params():
    return pltpu.CompilerParams(vmem_limit_bytes=VMEM_MIB << 20)


def cost(flops, moved):
    return pl.CostEstimate(flops=int(flops), bytes_accessed=int(moved), transcendentals=0)


def dot(a, b, contract=NN):
    return lax.dot_general(a, b, (contract, ((), ())), preferred_element_type=F32)


def state_body(k_ref, v_ref, total_ref, sent_ref, prefix_ref, vt_ref):
    for pair in range(2):
        cols = slice(pair * HEAD, (pair + 1) * HEAD)
        vt = jnp.transpose(v_ref[:, cols])
        vt_ref[cols, :] = vt
        total = None
        for c in range(CHUNKS):
            rows = slice(c * CHUNK, (c + 1) * CHUNK)
            part = dot(vt[:, rows], k_ref[rows, cols])
            total = part if total is None else total + part
            if c + 1 < CHUNKS:
                prefix_ref[pair, c] = total.astype(BF16)
        total_ref[pair] = total
        sent_ref[pair] = total.astype(BF16)


def states(keys, values):
    block = pl.BlockSpec((ROWS, 2 * HEAD), lambda i: (0, i))
    square = pl.BlockSpec((2, HEAD, HEAD), lambda i: (i, 0, 0))
    return pl.pallas_call(
        state_body,
        grid=(HEADS // 2,),
        in_specs=[block, block],
        out_specs=[
            square,
            square,
            pl.BlockSpec((2, CHUNKS - 1, HEAD, HEAD), lambda i: (i, 0, 0, 0)),
            pl.BlockSpec((2 * HEAD, ROWS), lambda i: (i, 0)),
        ],
        out_shape=[
            jax.ShapeDtypeStruct((HEADS, HEAD, HEAD), F32),
            jax.ShapeDtypeStruct((HEADS, HEAD, HEAD), BF16),
            jax.ShapeDtypeStruct((HEADS, CHUNKS - 1, HEAD, HEAD), BF16),
            jax.ShapeDtypeStruct((HEADS * HEAD, ROWS), BF16),
        ],
        compiler_params=params(),
        cost_estimate=cost(1e9, 14 << 20),
        name="states",
    )(keys, values)


def quarter_of(number, s):
    side, sub = divmod(number, 2)
    return (s[0] ^ side) * 2 + (s[1] ^ sub)


def local_body(number, s_ref, q_ref, k_ref, vt_ref, prefix_ref, first_ref, gate0_ref, gate1_ref, out_ref):
    within = lax.rem(quarter_of(number, s_ref) * QUARTER + pl.program_id(0), HEADS)
    causal = lax.broadcasted_iota(jnp.int32, (CHUNK, CHUNK), 0) <= lax.broadcasted_iota(
        jnp.int32, (CHUNK, CHUNK), 1
    )
    w0 = gate0_ref[pl.ds(within, 1), :]
    w1 = gate1_ref[pl.ds(within, 1), :]
    for c in range(CHUNKS):
        rows = slice(c * CHUNK, (c + 1) * CHUNK)
        q = q_ref[rows, :]
        scores = dot(k_ref[rows, :], q, NT)
        scores = jnp.where(causal, scores, 0.0).astype(BF16)
        mixed = dot(vt_ref[:, rows], scores)
        if c:
            both = jnp.concatenate([prefix_ref[0, c - 1], first_ref[0]], axis=0)
            both = dot(both, q, NT)
            mixed = mixed + both[:HEAD]
            level = both[HEAD:]
        else:
            level = dot(first_ref[0], q, NT)
        out_ref[:, rows] = mixed * w0[:, rows] + level * w1[:, rows]


def local(number, scalars, queries, keys, vt, prefix, first, gate):
    where = lambda i, s: quarter_of(number, s) * QUARTER + i
    block = pl.BlockSpec((ROWS, HEAD), lambda i, s: (0, where(i, s)))
    return pl.pallas_call(
        functools.partial(local_body, number),
        grid_spec=pltpu.PrefetchScalarGridSpec(
            num_scalar_prefetch=1,
            grid=(QUARTER,),
            in_specs=[
                block,
                block,
                pl.BlockSpec((HEAD, ROWS), lambda i, s: (where(i, s), 0)),
                pl.BlockSpec((1, CHUNKS - 1, HEAD, HEAD), lambda i, s: (where(i, s), 0, 0, 0)),
                pl.BlockSpec((1, HEAD, HEAD), lambda i, s: (where(i, s), 0, 0)),
                pl.BlockSpec((HEADS, ROWS), lambda i, s: (0, 0)),
                pl.BlockSpec((HEADS, ROWS), lambda i, s: (1, 0)),
            ],
            out_specs=pl.BlockSpec((HEAD, ROWS), lambda i, s: (i, 0)),
        ),
        out_shape=jax.ShapeDtypeStruct((QUARTER * HEAD, ROWS), F32),
        compiler_params=params(),
        cost_estimate=cost(2e9, 6 << 20),
        name=f"local{number}",
    )(scalars, queries, keys, vt, prefix, first, gate, gate)


def norm_body(count, s_ref, *refs):
    gate_ref, gain_ref, out_ref = refs[-3:]
    for number in range(4):
        q_ref, a_ref, *buckets = refs[number * (2 + count) : (number + 1) * (2 + count)]
        head = quarter_of(number, s_ref) * QUARTER + pl.program_id(0)
        squares = jnp.concatenate([b[0] for b in buckets], axis=0)
        gain = gain_ref[pl.ds(head, 1), :]
        weights = [gate_ref[pl.ds((n + 2) * HEADS + head, 1), :] for n in range(count)]
        for c in range(CHUNKS):
            rows = slice(c * CHUNK, (c + 1) * CHUNK)
            products = dot(squares, q_ref[rows, :], NT)
            x = a_ref[:, rows]
            for n in range(count):
                x = x + products[n * HEAD : (n + 1) * HEAD] * weights[n][:, rows]
            mean = jnp.mean(x * x, axis=0, keepdims=True)
            x = jnp.transpose(x * lax.rsqrt(mean + EPSILON))
            cols = pl.ds(pl.multiple_of(head * HEAD, HEAD), HEAD)
            out_ref[rows, cols] = (x * gain).astype(BF16)


def normed(scalars, queries, attended, buckets, gate, gain):
    count = len(buckets[0])
    operands, specs = [], []
    for number in range(4):
        head = lambda i, s, number=number: (0, quarter_of(number, s) * QUARTER + i)
        operands += [queries, attended[number]]
        specs += [pl.BlockSpec((ROWS, HEAD), head), pl.BlockSpec((HEAD, ROWS), lambda i, s: (i, 0))]
        for array, index in buckets[number]:
            operands.append(array)
            specs.append(pl.BlockSpec((1, HEAD, HEAD), lambda i, s, index=index: (index(i, s), 0, 0)))
    return pl.pallas_call(
        functools.partial(norm_body, count),
        grid_spec=pltpu.PrefetchScalarGridSpec(
            num_scalar_prefetch=1,
            grid=(QUARTER,),
            in_specs=[
                *specs,
                pl.BlockSpec((GATES * HEADS, ROWS), lambda i, s: (0, 0)),
                pl.BlockSpec((HEADS, HEAD), lambda i, s: (0, 0)),
            ],
            out_specs=pl.BlockSpec((ROWS, HEADS * HEAD), lambda i, s: (0, 0)),
        ),
        out_shape=jax.ShapeDtypeStruct((ROWS, HEADS * HEAD), BF16),
        compiler_params=params(),
        cost_estimate=cost(4e9, 18 << 20),
        name="normed",
    )(scalars, *operands, gate, gain)


def project_body(n_ref, w_ref, out_ref):
    out_ref[...] = dot(n_ref[...], w_ref[...]).astype(BF16)


def project(rows, weight):
    tile = 256
    return pl.pallas_call(
        project_body,
        grid=(HEADS * HEAD // tile,),
        in_specs=[
            pl.BlockSpec((ROWS, HEADS * HEAD), lambda i: (0, 0)),
            pl.BlockSpec((HEADS * HEAD, tile), lambda i: (0, i)),
        ],
        out_specs=pl.BlockSpec((ROWS, tile), lambda i: (0, i)),
        out_shape=jax.ShapeDtypeStruct((ROWS, HEADS * HEAD), BF16),
        compiler_params=params(),
        cost_estimate=cost(8e9, 16 << 20),
        name="project",
    )(rows, weight)


def from_partner(value, axis, bit):
    mask = 2**bit
    pairs = [(source, source ^ mask) for source in range(lax.axis_size(axis))]
    return lax.ppermute(value, axis, pairs)


def plain_bucket(array, number):
    return array, lambda i, s: (s[1] ^ (number % 2)) * QUARTER + i


def batch_bucket(array, number, at, size):
    return array, lambda i, s: (number % 2) * size * QUARTER + at * QUARTER + i


def shards(queries, keys, values, level_gate, norm_gain, out_weight):
    position = lax.axis_index("ctx")
    levels = lax.axis_size("ctx").bit_length() - 1
    core = position & 1
    near = position >> 1 & 1
    scalars = jnp.stack([core, near]).astype(jnp.int32)
    whole_weight = lax.all_gather(out_weight, "ctx", axis=0, tiled=True)
    bits = position >> jnp.arange(levels, dtype=jnp.int32) & 1
    present = jnp.concatenate([jnp.ones((1,), F32), bits.astype(F32)])
    gate = level_gate.T.astype(F32) * jnp.repeat(present, HEADS)[:, None]
    total, sent, prefix, vt = states(keys, values)
    first = from_partner(sent, "ctx", 0)
    running = lax.dynamic_slice_in_dim(total, core * HALF, HALF) + lax.dynamic_slice_in_dim(
        first, core * HALF, HALF
    ).astype(F32)
    attended = []
    buckets = [[] for _ in range(4)]
    batch = []
    for level in range(1, levels):
        outgoing = running.astype(BF16)
        if level <= 4:
            if level > 2:
                outgoing, q, attended[level - 3] = lax.optimization_barrier(
                    (outgoing, queries, attended[level - 3])
                )
            else:
                outgoing, q = lax.optimization_barrier((outgoing, queries))
            attended.append(local(level - 1, scalars, q, keys, vt, prefix, first, gate))
        elif level - 3 < 4:
            outgoing, attended[level - 3] = lax.optimization_barrier((outgoing, attended[level - 3]))
        received = from_partner(outgoing, "ctx", level)
        if level == 1:
            other = from_partner(received, "ctx", 0)
            for number in range(4):
                buckets[number].append(plain_bucket((received, other)[number // 2], number))
            running = lax.dynamic_slice_in_dim(running, near * QUARTER, QUARTER) + lax.dynamic_slice_in_dim(
                received, near * QUARTER, QUARTER
            ).astype(F32)
            continue
        batch.append(received)
        if level % 2 or level + 1 == levels:
            size = len(batch)
            here = jnp.concatenate(batch) if size > 1 else batch[0]
            chip = jnp.concatenate([here, from_partner(here, "ctx", 1)])
            other = from_partner(chip, "ctx", 0)
            for at in range(size):
                for number in range(4):
                    buckets[number].append(batch_bucket((chip, other)[number // 2], number, at, size))
            batch = []
        if level + 1 < levels:
            running = running + received.astype(F32)
    gain = norm_gain.reshape(HEADS, HEAD)
    rows = normed(scalars, queries, attended, buckets, gate, gain)
    return project(rows, whole_weight)


def solution(mesh):
    placed = (P("ctx", None), P("ctx", None), P("ctx", None), P("ctx", None), P(), P("ctx", None))
    return jax.shard_map(
        shards, mesh=mesh, in_specs=placed, out_specs=P("ctx", None), check_vma=False
    )
```

```python
import functools

import jax
import jax.numpy as jnp
from jax import lax
from jax.experimental import pallas as pl
from jax.experimental.pallas import tpu as pltpu
from jax.sharding import PartitionSpec as P


HEADS = 16
HEAD = 128
GATES = 8
HALF = HEADS // 2
QUARTER = HEADS // 4
ROWS = 1024
CHUNK = 256
CHUNKS = ROWS // CHUNK
EPSILON = 1e-06
VMEM_MIB = 60
F32 = jnp.float32
BF16 = jnp.bfloat16
NN = ((1,), (0,))
NT = ((1,), (1,))


def params():
    return pltpu.CompilerParams(vmem_limit_bytes=VMEM_MIB << 20)


def cost(flops, moved):
    return pl.CostEstimate(flops=int(flops), bytes_accessed=int(moved), transcendentals=0)


def dot(a, b, contract=NN):
    return lax.dot_general(a, b, (contract, ((), ())), preferred_element_type=F32)


def state_body(k_ref, v_ref, total_ref, sent_ref, prefix_ref, vt_ref):
    for pair in range(2):
        cols = slice(pair * HEAD, (pair + 1) * HEAD)
        vt = jnp.transpose(v_ref[:, cols])
        vt_ref[cols, :] = vt
        total = None
        for c in range(CHUNKS):
            rows = slice(c * CHUNK, (c + 1) * CHUNK)
            part = dot(vt[:, rows], k_ref[rows, cols])
            total = part if total is None else total + part
            if c + 1 < CHUNKS:
                prefix_ref[pair, c] = total.astype(BF16)
        total_ref[pair] = total
        sent_ref[pair] = total.astype(BF16)


def states(keys, values):
    block = pl.BlockSpec((ROWS, 2 * HEAD), lambda i: (0, i))
    square = pl.BlockSpec((2, HEAD, HEAD), lambda i: (i, 0, 0))
    return pl.pallas_call(
        state_body,
        grid=(HEADS // 2,),
        in_specs=[block, block],
        out_specs=[
            square,
            square,
            pl.BlockSpec((2, CHUNKS - 1, HEAD, HEAD), lambda i: (i, 0, 0, 0)),
            pl.BlockSpec((2 * HEAD, ROWS), lambda i: (i, 0)),
        ],
        out_shape=[
            jax.ShapeDtypeStruct((HEADS, HEAD, HEAD), F32),
            jax.ShapeDtypeStruct((HEADS, HEAD, HEAD), BF16),
            jax.ShapeDtypeStruct((HEADS, CHUNKS - 1, HEAD, HEAD), BF16),
            jax.ShapeDtypeStruct((HEADS * HEAD, ROWS), BF16),
        ],
        compiler_params=params(),
        cost_estimate=cost(1e9, 14 << 20),
        name="states",
    )(keys, values)


def quarter_of(number, s):
    side, sub = divmod(number, 2)
    return (s[0] ^ side) * 2 + (s[1] ^ sub)


def local_body(number, s_ref, q_ref, k_ref, vt_ref, prefix_ref, first_ref, gate0_ref, gate1_ref, out_ref):
    within = lax.rem(quarter_of(number, s_ref) * QUARTER + pl.program_id(0), HEADS)
    causal = lax.broadcasted_iota(jnp.int32, (CHUNK, CHUNK), 0) <= lax.broadcasted_iota(
        jnp.int32, (CHUNK, CHUNK), 1
    )
    w0 = gate0_ref[pl.ds(within, 1), :]
    w1 = gate1_ref[pl.ds(within, 1), :]
    for c in range(CHUNKS):
        rows = slice(c * CHUNK, (c + 1) * CHUNK)
        q = q_ref[rows, :]
        scores = dot(k_ref[rows, :], q, NT)
        scores = jnp.where(causal, scores, 0.0).astype(BF16)
        mixed = dot(vt_ref[:, rows], scores)
        if c:
            both = jnp.concatenate([prefix_ref[0, c - 1], first_ref[0]], axis=0)
            both = dot(both, q, NT)
            mixed = mixed + both[:HEAD]
            level = both[HEAD:]
        else:
            level = dot(first_ref[0], q, NT)
        out_ref[:, rows] = mixed * w0[:, rows] + level * w1[:, rows]


def local(number, scalars, queries, keys, vt, prefix, first, gate):
    where = lambda i, s: quarter_of(number, s) * QUARTER + i
    block = pl.BlockSpec((ROWS, HEAD), lambda i, s: (0, where(i, s)))
    return pl.pallas_call(
        functools.partial(local_body, number),
        grid_spec=pltpu.PrefetchScalarGridSpec(
            num_scalar_prefetch=1,
            grid=(QUARTER,),
            in_specs=[
                block,
                block,
                pl.BlockSpec((HEAD, ROWS), lambda i, s: (where(i, s), 0)),
                pl.BlockSpec((1, CHUNKS - 1, HEAD, HEAD), lambda i, s: (where(i, s), 0, 0, 0)),
                pl.BlockSpec((1, HEAD, HEAD), lambda i, s: (where(i, s), 0, 0)),
                pl.BlockSpec((HEADS, ROWS), lambda i, s: (0, 0)),
                pl.BlockSpec((HEADS, ROWS), lambda i, s: (1, 0)),
            ],
            out_specs=pl.BlockSpec((HEAD, ROWS), lambda i, s: (i, 0)),
        ),
        out_shape=jax.ShapeDtypeStruct((QUARTER * HEAD, ROWS), F32),
        compiler_params=params(),
        cost_estimate=cost(2e9, 6 << 20),
    )(scalars, queries, keys, vt, prefix, first, gate, gate)


def final_body(count, s_ref, *refs):
    gate_ref, gain_ref, weight_ref, out_ref, normed_ref = refs[-5:]
    step = pl.program_id(0)

    @pl.when(step < QUARTER)
    def _():
        norm_heads(count, s_ref, refs[:-5], gate_ref, gain_ref, normed_ref)

    @pl.when(step >= QUARTER)
    def _():
        out_ref[...] = dot(normed_ref[...], weight_ref[...]).astype(BF16)


def norm_heads(count, s_ref, refs, gate_ref, gain_ref, out_ref):
    for number in range(4):
        q_ref, a_ref, *buckets = refs[number * (2 + count) : (number + 1) * (2 + count)]
        head = quarter_of(number, s_ref) * QUARTER + pl.program_id(0)
        squares = jnp.concatenate([b[0] for b in buckets], axis=0)
        gain = gain_ref[pl.ds(head, 1), :]
        weights = [gate_ref[pl.ds((n + 2) * HEADS + head, 1), :] for n in range(count)]
        for c in range(CHUNKS):
            rows = slice(c * CHUNK, (c + 1) * CHUNK)
            products = dot(squares, q_ref[rows, :], NT)
            x = a_ref[:, rows]
            for n in range(count):
                x = x + products[n * HEAD : (n + 1) * HEAD] * weights[n][:, rows]
            mean = jnp.mean(x * x, axis=0, keepdims=True)
            x = jnp.transpose(x * lax.rsqrt(mean + EPSILON))
            cols = pl.ds(pl.multiple_of(head * HEAD, HEAD), HEAD)
            out_ref[rows, cols] = (x * gain).astype(BF16)


def final(scalars, queries, attended, buckets, gate, gain, weight):
    count = len(buckets[0])
    tile = 256
    early = lambda i: jnp.minimum(i, QUARTER - 1)
    late = lambda i, s: (0, jnp.maximum(i - QUARTER, 0))
    operands, specs = [], []
    for number in range(4):
        head = lambda i, s, number=number: (0, quarter_of(number, s) * QUARTER + early(i))
        operands += [queries, attended[number]]
        specs += [pl.BlockSpec((ROWS, HEAD), head), pl.BlockSpec((HEAD, ROWS), lambda i, s: (early(i), 0))]
        for array, index in buckets[number]:
            operands.append(array)
            specs.append(pl.BlockSpec((1, HEAD, HEAD), lambda i, s, index=index: (index(early(i), s), 0, 0)))
    return pl.pallas_call(
        functools.partial(final_body, count),
        grid_spec=pltpu.PrefetchScalarGridSpec(
            num_scalar_prefetch=1,
            grid=(QUARTER + HEADS * HEAD // tile,),
            in_specs=[
                *specs,
                pl.BlockSpec((GATES * HEADS, ROWS), lambda i, s: (0, 0)),
                pl.BlockSpec((HEADS, HEAD), lambda i, s: (0, 0)),
                pl.BlockSpec((HEADS * HEAD, tile), late),
            ],
            out_specs=pl.BlockSpec((ROWS, tile), late),
            scratch_shapes=[pltpu.VMEM((ROWS, HEADS * HEAD), BF16)],
        ),
        out_shape=jax.ShapeDtypeStruct((ROWS, HEADS * HEAD), BF16),
        compiler_params=params(),
        cost_estimate=cost(12e9, 30 << 20),
        name="final",
    )(scalars, *operands, gate, gain, weight)


def from_partner(value, axis, bit):
    mask = 2**bit
    pairs = [(source, source ^ mask) for source in range(lax.axis_size(axis))]
    return lax.ppermute(value, axis, pairs)


def plain_bucket(array, number):
    return array, lambda i, s: (s[1] ^ (number % 2)) * QUARTER + i


def batch_bucket(array, number, at, size):
    return array, lambda i, s: (number % 2) * size * QUARTER + at * QUARTER + i


def shards(queries, keys, values, level_gate, norm_gain, out_weight):
    position = lax.axis_index("ctx")
    levels = lax.axis_size("ctx").bit_length() - 1
    core = position & 1
    near = position >> 1 & 1
    scalars = jnp.stack([core, near]).astype(jnp.int32)
    whole_weight = lax.all_gather(out_weight, "ctx", axis=0, tiled=True)
    bits = position >> jnp.arange(levels, dtype=jnp.int32) & 1
    present = jnp.concatenate([jnp.ones((1,), F32), bits.astype(F32)])
    gate = level_gate.T.astype(F32) * jnp.repeat(present, HEADS)[:, None]
    total, sent, prefix, vt = states(keys, values)
    first = from_partner(sent, "ctx", 0)
    running = lax.dynamic_slice_in_dim(total, core * HALF, HALF) + lax.dynamic_slice_in_dim(
        first, core * HALF, HALF
    ).astype(F32)
    attended = []
    buckets = [[] for _ in range(4)]
    batch = []
    for level in range(1, levels):
        outgoing = running.astype(BF16)
        if level <= 4:
            if level > 2:
                outgoing, q, attended[level - 3] = lax.optimization_barrier(
                    (outgoing, queries, attended[level - 3])
                )
            else:
                outgoing, q = lax.optimization_barrier((outgoing, queries))
            attended.append(local(level - 1, scalars, q, keys, vt, prefix, first, gate))
        elif level - 3 < 4:
            outgoing, attended[level - 3] = lax.optimization_barrier((outgoing, attended[level - 3]))
        received = from_partner(outgoing, "ctx", level)
        if level == 1:
            other = from_partner(received, "ctx", 0)
            for number in range(4):
                buckets[number].append(plain_bucket((received, other)[number // 2], number))
            running = lax.dynamic_slice_in_dim(running, near * QUARTER, QUARTER) + lax.dynamic_slice_in_dim(
                received, near * QUARTER, QUARTER
            ).astype(F32)
            continue
        batch.append(received)
        if level in (4, levels - 1):
            size = len(batch)
            here = jnp.concatenate(batch) if size > 1 else batch[0]
            chip = jnp.concatenate([here, from_partner(here, "ctx", 1)])
            other = from_partner(chip, "ctx", 0)
            for at in range(size):
                for number in range(4):
                    buckets[number].append(batch_bucket((chip, other)[number // 2], number, at, size))
            batch = []
        if level + 1 < levels:
            running = running + received.astype(F32)
    gain = norm_gain.reshape(HEADS, HEAD)
    return final(scalars, queries, attended, buckets, gate, gain, whole_weight)


def solution(mesh):
    placed = (P("ctx", None), P("ctx", None), P("ctx", None), P("ctx", None), P(), P("ctx", None))

    return jax.shard_map(shards, mesh=mesh, in_specs=placed, out_specs=P("ctx", None), check_vma=False)
```

```python
import functools

import jax
import jax.numpy as jnp
from jax import lax
from jax.experimental import pallas as pl
from jax.experimental.pallas import tpu as pltpu
from jax.sharding import PartitionSpec as P


HEADS = 16
HEAD = 128
GATES = 8
HALF = HEADS // 2
QUARTER = HEADS // 4
ROWS = 1024
CHUNK = 256
CHUNKS = ROWS // CHUNK
EPSILON = 1e-06
VMEM_MIB = 60
F32 = jnp.float32
BF16 = jnp.bfloat16
NN = ((1,), (0,))
NT = ((1,), (1,))


def params():
    return pltpu.CompilerParams(vmem_limit_bytes=VMEM_MIB << 20)


def cost(flops, moved):
    return pl.CostEstimate(flops=int(flops), bytes_accessed=int(moved), transcendentals=0)


def dot(a, b, contract=NN):
    return lax.dot_general(a, b, (contract, ((), ())), preferred_element_type=F32)


def state_body(k_ref, v_ref, total_ref, sent_ref, prefix_ref, vt_ref):
    for pair in range(2):
        cols = slice(pair * HEAD, (pair + 1) * HEAD)
        vt = jnp.transpose(v_ref[:, cols])
        vt_ref[cols, :] = vt
        total = None
        for c in range(CHUNKS):
            rows = slice(c * CHUNK, (c + 1) * CHUNK)
            part = dot(vt[:, rows], k_ref[rows, cols])
            total = part if total is None else total + part
            if c + 1 < CHUNKS:
                prefix_ref[pair, c] = total.astype(BF16)
        total_ref[pair] = total
        sent_ref[pair] = total.astype(BF16)


def states(keys, values):
    block = pl.BlockSpec((ROWS, 2 * HEAD), lambda i: (0, i))
    square = pl.BlockSpec((2, HEAD, HEAD), lambda i: (i, 0, 0))
    return pl.pallas_call(
        state_body,
        grid=(HEADS // 2,),
        in_specs=[block, block],
        out_specs=[
            square,
            square,
            pl.BlockSpec((2, CHUNKS - 1, HEAD, HEAD), lambda i: (i, 0, 0, 0)),
            pl.BlockSpec((2 * HEAD, ROWS), lambda i: (i, 0)),
        ],
        out_shape=[
            jax.ShapeDtypeStruct((HEADS, HEAD, HEAD), F32),
            jax.ShapeDtypeStruct((HEADS, HEAD, HEAD), BF16),
            jax.ShapeDtypeStruct((HEADS, CHUNKS - 1, HEAD, HEAD), BF16),
            jax.ShapeDtypeStruct((HEADS * HEAD, ROWS), BF16),
        ],
        compiler_params=params(),
        cost_estimate=cost(1e9, 14 << 20),
        name="states",
    )(keys, values)


def quarter_of(number, s):
    side, sub = divmod(number, 2)
    return (s[0] ^ side) * 2 + (s[1] ^ sub)


def local_body(number, s_ref, q_ref, k_ref, vt_ref, prefix_ref, first_ref, gate0_ref, gate1_ref, out_ref):
    within = lax.rem(quarter_of(number, s_ref) * QUARTER + pl.program_id(0), HEADS)
    causal = lax.broadcasted_iota(jnp.int32, (CHUNK, CHUNK), 0) <= lax.broadcasted_iota(
        jnp.int32, (CHUNK, CHUNK), 1
    )
    w0 = gate0_ref[pl.ds(within, 1), :]
    w1 = gate1_ref[pl.ds(within, 1), :]
    for c in range(CHUNKS):
        rows = slice(c * CHUNK, (c + 1) * CHUNK)
        q = q_ref[rows, :]
        scores = dot(k_ref[rows, :], q, NT)
        scores = jnp.where(causal, scores, 0.0).astype(BF16)
        mixed = dot(vt_ref[:, rows], scores)
        if c:
            both = jnp.concatenate([prefix_ref[0, c - 1], first_ref[0]], axis=0)
            both = dot(both, q, NT)
            mixed = mixed + both[:HEAD]
            level = both[HEAD:]
        else:
            level = dot(first_ref[0], q, NT)
        out_ref[:, rows] = mixed * w0[:, rows] + level * w1[:, rows]


def local(number, scalars, queries, keys, vt, prefix, first, gate):
    where = lambda i, s: quarter_of(number, s) * QUARTER + i
    block = pl.BlockSpec((ROWS, HEAD), lambda i, s: (0, where(i, s)))
    return pl.pallas_call(
        functools.partial(local_body, number),
        grid_spec=pltpu.PrefetchScalarGridSpec(
            num_scalar_prefetch=1,
            grid=(QUARTER,),
            in_specs=[
                block,
                block,
                pl.BlockSpec((HEAD, ROWS), lambda i, s: (where(i, s), 0)),
                pl.BlockSpec((1, CHUNKS - 1, HEAD, HEAD), lambda i, s: (where(i, s), 0, 0, 0)),
                pl.BlockSpec((1, HEAD, HEAD), lambda i, s: (where(i, s), 0, 0)),
                pl.BlockSpec((HEADS, ROWS), lambda i, s: (0, 0)),
                pl.BlockSpec((HEADS, ROWS), lambda i, s: (1, 0)),
            ],
            out_specs=pl.BlockSpec((HEAD, ROWS), lambda i, s: (i, 0)),
        ),
        out_shape=jax.ShapeDtypeStruct((QUARTER * HEAD, ROWS), F32),
        compiler_params=params(),
        cost_estimate=cost(2e9, 6 << 20),
    )(scalars, queries, keys, vt, prefix, first, gate, gate)


def norm_body(count, s_ref, *refs):
    gate_ref, gain_ref, out_ref = refs[-3:]
    for number in range(4):
        q_ref, a_ref, *buckets = refs[number * (2 + count) : (number + 1) * (2 + count)]
        head = quarter_of(number, s_ref) * QUARTER + pl.program_id(0)
        squares = jnp.concatenate([b[0] for b in buckets], axis=0)
        gain = gain_ref[pl.ds(head, 1), :]
        weights = [gate_ref[pl.ds((n + 2) * HEADS + head, 1), :] for n in range(count)]
        for c in range(CHUNKS):
            rows = slice(c * CHUNK, (c + 1) * CHUNK)
            products = dot(squares, q_ref[rows, :], NT)
            x = a_ref[:, rows]
            for n in range(count):
                x = x + products[n * HEAD : (n + 1) * HEAD] * weights[n][:, rows]
            mean = jnp.mean(x * x, axis=0, keepdims=True)
            x = jnp.transpose(x * lax.rsqrt(mean + EPSILON))
            cols = pl.ds(pl.multiple_of(head * HEAD, HEAD), HEAD)
            out_ref[rows, cols] = (x * gain).astype(BF16)


def normed(scalars, queries, attended, buckets, gate, gain):
    count = len(buckets[0])
    operands, specs = [], []
    for number in range(4):
        head = lambda i, s, number=number: (0, quarter_of(number, s) * QUARTER + i)
        operands += [queries, attended[number]]
        specs += [pl.BlockSpec((ROWS, HEAD), head), pl.BlockSpec((HEAD, ROWS), lambda i, s: (i, 0))]
        for array, index in buckets[number]:
            operands.append(array)
            specs.append(pl.BlockSpec((1, HEAD, HEAD), lambda i, s, index=index: (index(i, s), 0, 0)))
    return pl.pallas_call(
        functools.partial(norm_body, count),
        grid_spec=pltpu.PrefetchScalarGridSpec(
            num_scalar_prefetch=1,
            grid=(QUARTER,),
            in_specs=[
                *specs,
                pl.BlockSpec((GATES * HEADS, ROWS), lambda i, s: (0, 0)),
                pl.BlockSpec((HEADS, HEAD), lambda i, s: (0, 0)),
            ],
            out_specs=pl.BlockSpec((ROWS, HEADS * HEAD), lambda i, s: (0, 0)),
        ),
        out_shape=jax.ShapeDtypeStruct((ROWS, HEADS * HEAD), BF16),
        compiler_params=params(),
        cost_estimate=cost(4e9, 18 << 20),
        name="normed",
    )(scalars, *operands, gate, gain)


def project_body(n_ref, w_ref, out_ref):
    out_ref[...] = dot(n_ref[...], w_ref[...]).astype(BF16)


def project(rows, weight):
    tile = 256
    return pl.pallas_call(
        project_body,
        grid=(HEADS * HEAD // tile,),
        in_specs=[
            pl.BlockSpec((ROWS, HEADS * HEAD), lambda i: (0, 0)),
            pl.BlockSpec((HEADS * HEAD, tile), lambda i: (0, i)),
        ],
        out_specs=pl.BlockSpec((ROWS, tile), lambda i: (0, i)),
        out_shape=jax.ShapeDtypeStruct((ROWS, HEADS * HEAD), BF16),
        compiler_params=params(),
        cost_estimate=cost(8e9, 16 << 20),
        name="project",
    )(rows, weight)


def from_partner(value, axis, bit):
    mask = 2**bit
    pairs = [(source, source ^ mask) for source in range(lax.axis_size(axis))]
    return lax.ppermute(value, axis, pairs)


def plain_bucket(array, number):
    return array, lambda i, s: (s[1] ^ (number % 2)) * QUARTER + i


def batch_bucket(array, number, at, size):
    return array, lambda i, s: (number % 2) * size * QUARTER + at * QUARTER + i


def shards(queries, keys, values, level_gate, norm_gain, out_weight):
    position = lax.axis_index("ctx")
    levels = lax.axis_size("ctx").bit_length() - 1
    core = position & 1
    near = position >> 1 & 1
    scalars = jnp.stack([core, near]).astype(jnp.int32)
    whole_weight = lax.all_gather(out_weight, "ctx", axis=0, tiled=True)
    bits = position >> jnp.arange(levels, dtype=jnp.int32) & 1
    present = jnp.concatenate([jnp.ones((1,), F32), bits.astype(F32)])
    gate = level_gate.T.astype(F32) * jnp.repeat(present, HEADS)[:, None]
    total, sent, prefix, vt = states(keys, values)
    first = from_partner(sent, "ctx", 0)
    running = lax.dynamic_slice_in_dim(total, core * HALF, HALF) + lax.dynamic_slice_in_dim(
        first, core * HALF, HALF
    ).astype(F32)
    attended = []
    buckets = [[] for _ in range(4)]
    batch = []
    for level in range(1, levels):
        outgoing = running.astype(BF16)
        if level <= 4:
            if level > 2:
                outgoing, q, attended[level - 3] = lax.optimization_barrier(
                    (outgoing, queries, attended[level - 3])
                )
            else:
                outgoing, q = lax.optimization_barrier((outgoing, queries))
            attended.append(local(level - 1, scalars, q, keys, vt, prefix, first, gate))
        elif level - 3 < 4:
            outgoing, attended[level - 3] = lax.optimization_barrier((outgoing, attended[level - 3]))
        received = from_partner(outgoing, "ctx", level)
        if level == 1:
            other = from_partner(received, "ctx", 0)
            for number in range(4):
                buckets[number].append(plain_bucket((received, other)[number // 2], number))
            running = lax.dynamic_slice_in_dim(running, near * QUARTER, QUARTER) + lax.dynamic_slice_in_dim(
                received, near * QUARTER, QUARTER
            ).astype(F32)
            continue
        batch.append(received)
        if level + 1 == levels:
            beside = from_partner(received, "ctx", 1)
            pieces = [received, beside]
            pieces += [from_partner(received, "ctx", 0), from_partner(beside, "ctx", 0)]
            for number in range(4):
                buckets[number].append((pieces[number], lambda i, s: i))
        elif level in (3, 4, 5):
            size = len(batch)
            here = jnp.concatenate(batch) if size > 1 else batch[0]
            chip = jnp.concatenate([here, from_partner(here, "ctx", 1)])
            other = from_partner(chip, "ctx", 0)
            for at in range(size):
                for number in range(4):
                    buckets[number].append(batch_bucket((chip, other)[number // 2], number, at, size))
            batch = []
        if level + 1 < levels:
            running = running + received.astype(F32)
    gain = norm_gain.reshape(HEADS, HEAD)
    rows = normed(scalars, queries, attended, buckets, gate, gain)
    return project(rows, whole_weight)


def solution(mesh):
    placed = (P("ctx", None), P("ctx", None), P("ctx", None), P("ctx", None), P(), P("ctx", None))

    return jax.shard_map(shards, mesh=mesh, in_specs=placed, out_specs=P("ctx", None), check_vma=False)
```
